32 devices in a mesh: dom: 32 (over z, y, x, core).
Axes of the slice: x: 2, y: 2, z: 4, core: 2. Of those that a mesh axis runs over, the one named last changes fastest.
Arguments:
- rest_pos: float32 [3, 131072], P(None, 'dom'), may hold values from -6 to 6
- displacement: float32 [3, 131072], P(None, 'dom'), may hold values from -3 to 3
- velocity: float32 [3, 131072], P(None, 'dom'), may hold values from -6 to 6
- ext_force: float32 [3, 131072], P(None, 'dom'), may hold values from -6 to 6
- node_mass: float32 [131072], P('dom'), may hold values from 0.5 to 2
- body_accel: float32 [3], replicated, may hold values from -2 to 2
- connectivity: int32 [8, 131072], P(None, 'dom'), may hold values from 0 to 4095
- elem_material: int32 [1024], P('dom'), may hold values from 0 to 7
- stiffness: float32 [8, 24, 24], replicated, may hold values from -1.25 to 1.25
- shared_nodes: int32 [32, 5, 128], P('dom'), may hold values from 0 to 4095, as said below
- contact_slave: int32 [65536], P('dom'), may hold values from 0 to 4095
- contact_owner: int32 [65536, 1], P('dom'), may hold values from 0 to 31; in each aligned block of 2048 rows (0 to 2047, 2048 to 4095, ...) at most 256 rows name the same one
- contact_master: int32 [65536], P('dom'), may hold values from 0 to 4095
- contact_normal: float32 [3, 65536], P(None, 'dom'), may hold values from -4 to 4
- part_of_node: int32 [131072], P('dom'), may hold values from 0 to 799
- part_mass: float32 [400], replicated, may hold values from 81 to 327
- part_center: float32 [3, 400], replicated, may hold values from -1 to 1
- part_inertia: float32 [3, 400], replicated, may hold values from 81 to 327
Outputs:
- nodal_velocity: float32 [3, 131072], P(None, 'dom')
- part_motion: float32 [6, 400], replicated
The draws below stay inside these ranges and needn't reach their ends.
Inputs may be any that keep to these rules, and one draw needn't show every extreme that they name: `connectivity`: offsets are taken modulo 4096 after adding the element's own local number. `shared_nodes`: on each partition d the 5 x 128 entries are distinct interface copies; entry k of list b on d and entry k of list b on d XOR 2**b are copies of one node. `contact_slave`: slave indices are local copies of the contact's own partition. `contact_owner`: among the 2048 contacts of one partition no owner appears more than 256 times, and some owner appears exactly 256 times. `contact_master`: master indices are local copies of the owner partition. `part_of_node`: values of 400 or more mark copies of no rigid part.
All inputs are finite; a program needn't handle non-finite values.
Results may differ from the reference program's by a relative error of at most 0.0001.
Values sent between devices are 32-bit elements; how exact they have to be, the bound alone decides.
A program may use at most 128 MiB of HBM per device.

```python
import math
import jax
import jax.numpy as jnp
import numpy as np
from jax import lax

NODE_DEV = 4096
E_DEV = 4096
SH = 128
NBR = 5
C_DEV = 2048
CAP = 256
CYCLES = 3
MATS = 8
PARTS_SIZE = 400
DOMS = 32
NODES = 131072
ELEMS = 131072
BLOCKS = 1024
CONTACTS = 65536


def draw_shared_nodes(key, part):
    domain_keys = jax.random.split(key, DOMS)
    orders = jax.vmap(lambda one_key: jax.random.permutation(one_key, NODE_DEV))(domain_keys)
    return orders[:, :NBR * SH].reshape(DOMS, NBR, SH).astype(jnp.int32)


def with_ends(drawn, stream_key, low, largest):
    longest = drawn.shape.index(max(drawn.shape))
    spots = []
    for shift in (0, 1):
        where = [jax.random.randint(jax.random.fold_in(stream_key, axis), (), 0, length) for axis, length in enumerate(drawn.shape)]
        where[longest] = (where[longest] + shift) % drawn.shape[longest]
        spots.append(tuple(where))
    return drawn.at[spots[0]].set(low).at[spots[1]].set(largest)


def levels(key, shape, cuts, smallest, largest):
    level = 1.0
    for dim, shards_of in cuts:
        steps = jax.random.uniform(jax.random.fold_in(jax.random.fold_in(key, 6), dim), (shards_of,), jnp.float32, smallest / len(cuts), largest / len(cuts))
        level = level * jnp.repeat(jnp.exp(steps), shape[dim] // shards_of).reshape((-1,) + (1,) * (len(shape) - 1 - dim))
    return level


def assign_block(key, own, number, rows, count, top, bound, lean):
    ranking = jax.random.permutation(key, count)
    heavy_load, common = load_shares(count, rows * top, bound, lean, True), load_shares(count, rows * top, bound, lean, False)
    places = jnp.arange(count)

    def named(tallies, rotation):
        used = int((tallies > 0).sum())
        fixed = max(1, used // 4)
        shifted = fixed + (places - fixed + rotation * (used - fixed)) % max(1, count - fixed)
        return jnp.zeros((count,), jnp.int32).at[ranking[jnp.where(places < fixed, places, shifted)]].set(jnp.asarray(tallies, jnp.int32))

    tallies = jnp.where(number % 4 == 0, named(heavy_load, number // 4), named(common, number - number // 4 - 1))
    mixed = jax.random.permutation(jax.random.fold_in(own, 3), count)
    donor, receiver = mixed[0:count // 2 * 2:2], mixed[1:count // 2 * 2:2]
    slack = jnp.minimum(tallies[donor] - 1, bound - tallies[receiver]) // 2
    slack = jnp.where((donor == ranking[0]) | (receiver == ranking[0]) | (tallies[receiver] == 0), 0, jnp.maximum(slack, 0))
    shifted = jax.random.randint(jax.random.fold_in(own, 4), (count // 2,), 0, 1 << 20) % (slack + 1)
    tallies = tallies.at[donor].add(-shifted).at[receiver].add(shifted)
    labels = jnp.searchsorted(jnp.cumsum(tallies), jnp.arange(rows * top), side="right").astype(jnp.int32)
    listing = labels.reshape(top, rows).T
    listing = listing[jax.random.permutation(jax.random.fold_in(own, 1), rows)]
    rotation = jax.random.randint(jax.random.fold_in(own, 2), (rows, 1), 0, top)
    return jnp.take_along_axis(listing, (jnp.arange(top)[None, :] + rotation) % top, axis=1)


def load_shares(amount, total, most, lean, full):
    loads = [(1 << 20) // math.isqrt(standing ** lean) + 1 for standing in range(1, amount + 1)]
    largest = most if full else min(most, max(-(-total // amount), total * loads[0] // sum(loads)))
    least = 1 if total - largest >= amount - 1 else 0
    given, surplus = [largest] + [least] * (amount - 1), total - largest - least * (amount - 1)
    while surplus > 0:
        movable = [i for i in range(1, amount) if given[i] < largest] or [i for i in range(1, amount) if given[i] < most]
        pool, budget = sum([loads[i] for i in movable]), surplus
        for i in movable:
            more = min(most - given[i], max(1, budget * loads[i] // pool), surplus)
            given[i] = given[i] + more
            surplus = surplus - more
    return np.array(given)


def centred(rng, shape, spread, bound, cuts=(), kind=jnp.bfloat16):
    result = spread * jax.random.normal(rng, shape, jnp.float32)
    if cuts:
        result = result * levels(rng, shape, cuts, -0.22, 0.18)
    return jnp.clip(result, -bound, bound).astype(kind)


def setup_inputs(seed: int = 0) -> dict:
    keys = jax.random.split(jax.random.key(seed), 19)
    rest_pos = centred(keys[0], (3, NODES), 1.0, 6.0, ((1, 32),), jnp.float32)
    displacement = centred(keys[1], (3, NODES), 0.2, 3.0, ((1, 32),), jnp.float32)
    velocity = centred(keys[2], (3, NODES), 1.0, 6.0, ((1, 32),), jnp.float32)
    ext_force = centred(keys[3], (3, NODES), 1.0, 6.0, ((1, 32),), jnp.float32)
    node_mass = jnp.clip(jnp.exp(math.log(2.0) - 1.3862944 * jax.random.uniform(keys[4], (NODES,), jnp.float32) ** levels(keys[4], (NODES,), ((0, 32),), -0.2, 0.2)), 0.5, 2.0)
    body_accel = jnp.clip(jax.random.uniform(keys[5], (3,), jnp.float32, -2.0, 2.0), -2.0, 2.0)
    connectivity = with_ends(jax.random.randint(keys[6], (8, ELEMS), 0, min(NODE_DEV, 16368)), jax.random.fold_in(keys[6], 1), 0, (min(NODE_DEV, 16368)) - 1).astype(jnp.int32)
    elem_material = with_ends(jax.random.randint(keys[7], (BLOCKS,), 0, MATS), jax.random.fold_in(keys[7], 1), 0, MATS - 1).astype(jnp.int32)
    stiffness = centred(keys[8], (MATS, 24, 24), 24 ** -0.5, 1.25, (), jnp.float32)
    shared_nodes = draw_shared_nodes(jax.random.fold_in(keys[18], 71), 0)
    contact_slave = with_ends(jax.random.randint(keys[10], (CONTACTS,), 0, NODE_DEV), jax.random.fold_in(keys[10], 1), 0, NODE_DEV - 1).astype(jnp.int32)
    contact_owner_keys = jax.random.split(jax.random.fold_in(keys[11], 1), CONTACTS // C_DEV)
    contact_owner_turns = jax.random.permutation(jax.random.fold_in(keys[11], 3), CONTACTS // C_DEV)
    contact_owner = jax.vmap(lambda own, number: assign_block(jax.random.fold_in(keys[11], 2), own, number, C_DEV, DOMS, 1, CAP, 2))(contact_owner_keys, contact_owner_turns).reshape((CONTACTS, 1))
    contact_master = with_ends(jax.random.randint(keys[12], (CONTACTS,), 0, NODE_DEV), jax.random.fold_in(keys[12], 1), 0, NODE_DEV - 1).astype(jnp.int32)
    contact_normal = centred(keys[13], (3, CONTACTS), 0.6, 4.0, ((1, 32),), jnp.float32)
    part_of_node = with_ends(jax.random.randint(keys[14], (NODES,), 0, 2 * PARTS_SIZE), jax.random.fold_in(keys[14], 1), 0, (2 * PARTS_SIZE) - 1).astype(jnp.int32)
    part_mass = jnp.clip(jnp.exp(jax.random.uniform(keys[15], (PARTS_SIZE,), jnp.float32, math.log(81.0), math.log(327.0))), 81.0, 327.0)
    part_center = jnp.clip(jax.random.uniform(keys[16], (3, PARTS_SIZE), jnp.float32, -1.0, 1.0), -1.0, 1.0)
    part_inertia = jnp.clip(jnp.exp(jax.random.uniform(keys[17], (3, PARTS_SIZE), jnp.float32, math.log(81.0), math.log(327.0))), 81.0, 327.0)
    return dict(rest_pos=rest_pos, displacement=displacement, velocity=velocity, ext_force=ext_force, node_mass=node_mass, body_accel=body_accel, connectivity=connectivity, elem_material=elem_material, stiffness=stiffness, shared_nodes=shared_nodes, contact_slave=contact_slave, contact_owner=contact_owner, contact_master=contact_master, contact_normal=contact_normal, part_of_node=part_of_node, part_mass=part_mass, part_center=part_center, part_inertia=part_inertia)


TIME_STEP = 0.1
DAMP_RATIO = 0.05
PENALTY = 2.0
GAP_WIDTH = 0.5
CONTACT_DAMP = 0.2


def element_forces(corners, material, stiffness, nodal_field):
    blocks = corners.shape[1] // 128
    gathered = nodal_field[:, corners].reshape(24, blocks, 128)
    block_matrix = stiffness[material]
    forces = jnp.einsum("bij,jbk->ibk", block_matrix, gathered, precision=lax.Precision.HIGHEST)
    return jnp.zeros_like(nodal_field).at[:, corners.reshape(-1)].add(forces.reshape(3, 8 * corners.shape[1]))


def contact_push(slave_pos, slave_vel, master_pos, master_vel, normal):
    gap_size = jnp.sum((slave_pos - master_pos) * normal, axis=0)
    closing = jnp.sum((slave_vel - master_vel) * normal, axis=0)
    push_size = PENALTY * GAP_WIDTH * jax.nn.softplus(-gap_size / GAP_WIDTH) - CONTACT_DAMP * closing
    return push_size[None] * normal


def cross_product(left, right):
    return jnp.stack([left[1] * right[2] - left[2] * right[1], left[2] * right[0] - left[0] * right[2], left[0] * right[1] - left[1] * right[0]])


def by_domain(array_in):
    return array_in.reshape(array_in.shape[0], DOMS, NODE_DEV).transpose(1, 0, 2)


def to_global(array_in):
    return array_in.transpose(1, 0, 2).reshape(array_in.shape[1], NODES)


def take_columns(values_one, index_one):
    return values_one[:, index_one]


def add_columns(values_one, index_one, added_one):
    return values_one.at[:, index_one].add(added_one)


def reference(rest_pos, displacement, velocity, ext_force, node_mass, body_accel, connectivity, elem_material, stiffness, shared_nodes, contact_slave, contact_owner, contact_master, contact_normal, part_of_node, part_mass, part_center, part_inertia):
    displaced = by_domain(displacement)
    speeds = by_domain(velocity)
    applied = by_domain(ext_force)
    masses = node_mass.reshape(DOMS, 1, NODE_DEV)
    local_elem = jnp.arange(E_DEV, dtype=jnp.int32)
    corners = (connectivity.reshape(8, DOMS, E_DEV).transpose(1, 0, 2) + local_elem[None, None, :]) % NODE_DEV
    material = elem_material.reshape(DOMS, E_DEV // 128)
    shared_flat = shared_nodes.reshape(DOMS, NBR * SH)
    domain_ids = jnp.arange(DOMS, dtype=jnp.int32)
    accel_column = body_accel[None, :, None]

    def one_domain(inputs):
        return element_forces(inputs[0], inputs[1], stiffness, inputs[2])

    assembled = jnp.zeros_like(displaced)
    for cycle_index in range(CYCLES):
        internal = lax.map(one_domain, (corners, material, displaced + DAMP_RATIO * speeds))
        own_values = jax.vmap(take_columns)(internal, shared_flat).reshape(DOMS, 3, NBR, SH)
        pieces = [own_values[domain_ids ^ (1 << bit_number), :, bit_number] for bit_number in range(NBR)]
        received = jnp.stack(pieces, axis=2).reshape(DOMS, 3, NBR * SH)
        assembled = jax.vmap(add_columns)(internal, shared_flat, received)
        speeds = speeds + TIME_STEP * ((applied - assembled) / masses - accel_column)
        displaced = displaced + TIME_STEP * speeds

    positions = to_global(by_domain(rest_pos) + displaced)
    speeds_all = to_global(speeds)
    last_internal = to_global(assembled)
    contact_domain = jnp.arange(CONTACTS, dtype=jnp.int32) // C_DEV
    slave_node = contact_domain * NODE_DEV + contact_slave
    master_node = contact_owner[:, 0] * NODE_DEV + contact_master
    pushed = contact_push(positions[:, slave_node], speeds_all[:, slave_node], positions[:, master_node], speeds_all[:, master_node], contact_normal)
    contact = jnp.zeros_like(positions).at[:, slave_node].add(pushed).at[:, master_node].add(-pushed)
    nodal_velocity = speeds_all + TIME_STEP * contact / node_mass[None]
    net_force = ext_force - last_internal + contact - node_mass[None] * body_accel[:, None]

    part_index = jnp.minimum(part_of_node, PARTS_SIZE)

    def segment_rows(columns_in):
        return jax.ops.segment_sum(columns_in.T, part_index, PARTS_SIZE + 1)[:PARTS_SIZE].T

    mass_moments = segment_rows(jnp.concatenate([node_mass[None], node_mass[None] * positions], 0))
    mass_total = part_mass + mass_moments[0]
    centre = (part_mass[None] * part_center + mass_moments[1:4]) / mass_total[None]
    centre_ext = jnp.concatenate([centre, jnp.zeros((3, 1), centre.dtype)], 1)
    lever_arm = positions - centre_ext[:, part_index]
    load_sums = segment_rows(jnp.concatenate([net_force, cross_product(lever_arm, net_force)], 0))
    part_motion = jnp.concatenate([load_sums[0:3] / mass_total[None], load_sums[3:6] / part_inertia], 0)
    return nodal_velocity, part_motion
```

```python
import functools

import jax
import jax.numpy as jnp
from jax import lax
from jax.experimental import pallas as pl
from jax.experimental.pallas import tpu as pltpu
from jax.sharding import PartitionSpec as P

CYCLES = 3
PARTS_SIZE = 400
TIME_STEP = 0.1
DAMP_RATIO = 0.05
PENALTY = 2.0
GAP_WIDTH = 0.5
CONTACT_DAMP = 0.2
L = 128
GROUP = 4
F32 = jnp.float32
BF16 = jnp.bfloat16
NT = (((1,), (1,)), ((), ()))


def lookup(tables, index):
    high = index >> 7
    low = index & 127
    found = [None] * len(tables[0])
    for r, rows in enumerate(tables):
        hit = high == r
        for c, row in enumerate(rows):
            got = jnp.take_along_axis(
                jnp.broadcast_to(row, index.shape), low, axis=1, mode="promise_in_bounds"
            )
            found[c] = got if found[c] is None else jnp.where(hit, got, found[c])
    return found


def table_rows(refs, rows):
    return [[ref(r) for ref in refs] for r in range(rows)]


def scatter_tile(index, values, rows, pieces, live=None):
    high = (index >> 7).astype(F32)
    low = (index & 127).astype(F32)
    sublane = lax.broadcasted_iota(jnp.int32, (max(rows, 16), L), 0).astype(F32).astype(BF16)
    place = lax.broadcasted_iota(jnp.int32, (L, L), 0).astype(F32).astype(BF16)
    one, zero = jnp.ones((), BF16), jnp.zeros((), BF16)
    parts = []
    for value in values:
        value = jnp.concatenate(value, 0) if isinstance(value, list) else value
        for p in range(pieces):
            piece = value.astype(BF16).astype(F32) if p + 1 < pieces else value
            parts.append(piece)
            value = value - piece
    left, right = [], []

    def spread(value, s, count):
        row = jnp.broadcast_to(value[s : s + 1, :], (16, L)).astype(BF16)
        return jnp.concatenate([row] * (count // 16), 0) if count > 16 else row

    for s in range(live or index.shape[0]):
        mine = sublane == spread(high, s, sublane.shape[0])
        left.append(jnp.concatenate(
            [jnp.where(mine, spread(part, s, sublane.shape[0]), zero) for part in parts], 0))
        right.append(jnp.where(place == spread(low, s, L), one, zero))
    return lax.dot_general(
        jnp.concatenate(left, 1), jnp.concatenate(right, 1), NT, preferred_element_type=F32
    )


def unstack(total, count, rows, pieces):
    out = []
    step = max(rows, 16)
    for c in range(count):
        base = c * pieces * step
        value = total[base : base + rows]
        for p in range(1, pieces):
            value = value + total[base + p * step : base + p * step + rows]
        out.append(value)
    return out


def advance(u, v, internal, received, shared, ext, mass, accel, rows, neighbours):
    added = unstack(scatter_tile(shared, received, rows, 2, neighbours), 3, rows, 2)
    assembled = [internal[c] + added[c] for c in range(3)]
    v = [v[c] + TIME_STEP * ((ext[c] - assembled[c]) / mass - accel[c]) for c in range(3)]
    u = [u[c] + TIME_STEP * v[c] for c in range(3)]
    return u, v, assembled


def by_part(rec_ref):
    return [[rec_ref[b, c : c + 1, :] for b in range(rec_ref.shape[0])] for c in range(3)]


def corner_rows(conn_ref, b, nodes):
    start = pl.multiple_of(b * L, L)
    local = lax.broadcasted_iota(jnp.int32, (conn_ref.shape[0], L), 1) + start
    return lax.rem(conn_ref[:, pl.ds(start, L)] + local, nodes)


def split_matrix(stiff_ref, matrix_ref):
    for m in range(stiff_ref.shape[0]):
        k = stiff_ref[m]
        k_hi = k.astype(BF16).astype(F32)
        matrix_ref[m] = jnp.concatenate(
            [k_hi, k_hi, k - k_hi, jnp.zeros((k.shape[0], 8), F32)], 1).astype(BF16)


def internal_forces(field, total, conn_ref, material_ref, matrix_ref):
    rows = field.shape[1]
    nodes = rows * L
    total[...] = jnp.zeros_like(total)
    blocks = conn_ref.shape[1] // L

    def forces(b):
        found = lookup(
            table_rows([lambda r, c=c: field[c, r : r + 1, :] for c in range(3)], rows),
            corner_rows(conn_ref, b, nodes))
        g = jnp.concatenate(found, 0)
        g_hi = g.astype(BF16).astype(F32)
        rhs = jnp.concatenate([g_hi, g - g_hi, g_hi, jnp.zeros((8, L), F32)], 0).astype(BF16)
        h = jnp.dot(matrix_ref[material_ref[b]], rhs, preferred_element_type=F32)
        return h[0:8], h[8:16], h[16:24]

    def group(i):
        each = [forces(i * GROUP + k) for k in range(GROUP)]
        return tuple(jnp.concatenate([h[c] for h in each], 0) for c in range(3))

    def add_group(i, held):
        index = jnp.concatenate(
            [corner_rows(conn_ref, i * GROUP + k, nodes) for k in range(GROUP)], 0)
        total[...] += scatter_tile(index, list(held), rows, 2)

    def step(i, held):
        coming = group(i)
        add_group(i - 1, held)
        return coming

    groups = blocks // GROUP
    add_group(groups - 1, lax.fori_loop(1, groups, step, group(0)))
    return unstack(total[...], 3, rows, 2)


def shared_index(shared_ref):
    neighbours = shared_ref.shape[1]
    return jnp.concatenate(
        [shared_ref[0], jnp.zeros((8 - neighbours, shared_ref.shape[2]), jnp.int32)], 0)


def coords(index):
    return {"dom": index}


def greet(peers):
    barrier = pltpu.get_barrier_semaphore()
    for peer in peers:
        pl.semaphore_signal(barrier, inc=1, device_id=coords(peer),
                            device_id_type=pl.DeviceIdType.MESH)


def greeted(peers):
    pl.semaphore_wait(pltpu.get_barrier_semaphore(), len(peers))


def send(source, target, send_sem, recv_sem, peer):
    return pltpu.make_async_remote_copy(
        src_ref=source, dst_ref=target, send_sem=send_sem, recv_sem=recv_sem,
        device_id=coords(peer), device_id_type=pl.DeviceIdType.MESH)


def flips(me, neighbours):
    return [me + (1 - 2 * ((me // 2**b) % 2)) * 2**b for b in range(neighbours)]


def own_copies(own, rec_ref, send_sem, recv_sem, peers):
    return [send(own.at[b], rec_ref.at[b], send_sem.at[b], recv_sem.at[b], peer)
            for b, peer in enumerate(peers)]


def assemble(internal, int_ref, field, own, shared, neighbours):
    rows = field.shape[1]
    for c in range(3):
        int_ref[c] = internal[c]
        field[c] = internal[c]
    found = lookup(
        table_rows([lambda r, c=c: field[c, r : r + 1, :] for c in range(3)], rows), shared)
    for b in range(neighbours):
        for c in range(3):
            own[b, c : c + 1, :] = found[c][b : b + 1, :]


def put_slots(ref, at, value, each):
    for d in range(ref.shape[0]):
        ref[d, at * each : (at + 1) * each, :] = value[d * each : (d + 1) * each]


def slot_tile(ref, at, tile, each):
    step = 8 // each
    return jnp.concatenate(
        [ref[tile * step + j, at * each : (at + 1) * each, :] for j in range(step)], 0)


def slots(owner_ref, master_ref, normal_ref, slot_ref, pay, each):
    domains = pay.shape[0]
    tiles = owner_ref.shape[0]
    cap = each * L
    slot_rows = domains * each
    domain = lax.broadcasted_iota(jnp.int32, (domains, L), 0)
    tri = (lax.broadcasted_iota(jnp.int32, (L, L), 0) <= lax.broadcasted_iota(
        jnp.int32, (L, L), 1)).astype(F32).astype(BF16)
    seen = jnp.zeros((domains, 1), F32)
    for t in range(tiles):
        owner = owner_ref[t : t + 1, :]
        hit = domain == jnp.broadcast_to(owner, (domains, L))
        hits = jnp.where(hit, 1.0, 0.0)
        upto = jnp.dot(hits.astype(BF16), tri, preferred_element_type=F32) + seen
        rank = jnp.sum(jnp.where(hit, upto, 0.0), axis=0, keepdims=True) - 1.0
        slot_ref[t : t + 1, :] = owner * cap + rank.astype(jnp.int32)
        seen = seen + jnp.sum(hits, axis=1, keepdims=True)
    acc = None
    for t in range(0, tiles, 8):
        sl = slice(t, t + 8)
        values = [normal_ref[c, sl, :] for c in range(3)] + [master_ref[sl, :].astype(F32) + 1.0]
        got = scatter_tile(slot_ref[sl, :], values, slot_rows, 2)
        acc = got if acc is None else acc + got
    for c, value in enumerate(unstack(acc, 4, slot_rows, 2)):
        put_slots(pay, c, value, each)


def first_body(each, u_ref, v_ref, conn_ref, shared_ref, material_ref, stiff_ref, owner_ref,
               master_ref, normal_ref, int_ref, rec_ref, matrix_ref, slot_ref, early_ref, field,
               total, own, pay, send_sem, recv_sem, pay_send, pay_recv, own_sem):
    neighbours = shared_ref.shape[1]
    domains = pay.shape[0]
    me = lax.axis_index("dom")
    peers = [lax.rem(me + apart, domains) for apart in range(1, domains)]
    greet(peers)
    slots(owner_ref, master_ref, normal_ref, slot_ref, pay, each)
    split_matrix(stiff_ref, matrix_ref)
    for c in range(3):
        field[c] = u_ref[c] + DAMP_RATIO * v_ref[c]
    greeted(peers)
    early = [pltpu.make_async_copy(pay.at[me], early_ref.at[me], own_sem)]
    early += [send(pay.at[peer], early_ref.at[me], pay_send.at[i], pay_recv.at[i], peer)
              for i, peer in enumerate(peers)]
    for copy in early:
        copy.start()
    internal = internal_forces(field, total, conn_ref, material_ref, matrix_ref)
    assemble(internal, int_ref, field, own, shared_index(shared_ref), neighbours)
    copies = own_copies(own, rec_ref, send_sem, recv_sem, flips(me, neighbours))
    for copy in copies:
        copy.start()
    for copy in copies + early:
        copy.wait()


def next_body(u_ref, v_ref, conn_ref, shared_ref, material_ref, matrix_ref, old_ref, got_ref,
              ext_ref, mass_ref, accel_ref, int_ref, rec_ref, un_ref, vn_ref, field, total, own,
              send_sem, recv_sem):
    neighbours = shared_ref.shape[1]
    rows = u_ref.shape[1]
    me = lax.axis_index("dom")
    peers = flips(me, neighbours)
    greet(peers)
    shared = shared_index(shared_ref)
    u, v, _ = advance(
        [u_ref[c] for c in range(3)], [v_ref[c] for c in range(3)],
        [old_ref[c] for c in range(3)], by_part(got_ref), shared,
        [ext_ref[c] for c in range(3)], mass_ref[...], [accel_ref[c] for c in range(3)],
        rows, neighbours)
    for c in range(3):
        un_ref[c] = u[c]
        vn_ref[c] = v[c]
        field[c] = u[c] + DAMP_RATIO * v[c]
    internal = internal_forces(field, total, conn_ref, material_ref, matrix_ref)
    assemble(internal, int_ref, field, own, shared, neighbours)
    greeted(peers)
    copies = own_copies(own, rec_ref, send_sem, recv_sem, peers)
    for copy in copies:
        copy.start()
    for copy in copies:
        copy.wait()


def state_rows(x_ref, v_ref, rows):
    return table_rows(
        [lambda r, c=c: x_ref[c, r : r + 1, :] for c in range(3)]
        + [lambda r, c=c: v_ref[c, r : r + 1, :] for c in range(3)], rows)


def pushed(gap, closing):
    z = -gap / GAP_WIDTH
    soft = jnp.maximum(z, 0.0) + jnp.log1p(jnp.exp(-jnp.abs(z)))
    return PENALTY * GAP_WIDTH * soft - CONTACT_DAMP * closing


def bit_groups(domains):
    bits = domains.bit_length() - 1
    groups, low = [], 0
    while low < bits:
        width = min(3, bits - low)
        if bits - low == 4:
            width = 2
        groups.append((low, width))
        low += width
    return groups


def last_body(each, u_ref, v_ref, shared_ref, old_ref, got_ref, ext_ref, mass_ref, accel_ref,
              rest_ref, slave_ref, slot_ref, normal_ref, early_ref, part_ref, pmass_ref,
              pcentre_ref, pinertia_ref, nv_ref, motion_ref, x_ref, vn_ref, pay, back, slave_side,
              master_side, table, vals, total, sums, first, arrived, *scratch):
    domains = pay.shape[0]
    groups = bit_groups(domains)
    held, (pay_send, pay_recv, own_sem, sum_send, sum_recv, sum_own) = (
        scratch[:len(groups) - 1], scratch[len(groups) - 1:])
    held = (first,) + tuple(held)
    rows = u_ref.shape[1]
    slot_rows = domains * each
    neighbours = shared_ref.shape[1]
    me = lax.axis_index("dom")
    peers = [lax.rem(me + apart, domains) for apart in range(1, domains)]
    greet(peers)
    u, v, assembled = advance(
        [u_ref[c] for c in range(3)], [v_ref[c] for c in range(3)],
        [old_ref[c] for c in range(3)], by_part(got_ref), shared_index(shared_ref),
        [ext_ref[c] for c in range(3)], mass_ref[...], [accel_ref[c] for c in range(3)],
        rows, neighbours)
    mass = mass_ref[...]
    for c in range(3):
        x_ref[c] = rest_ref[c] + u[c]
        vn_ref[c] = v[c]
        vals[4 + c] = ext_ref[c] - assembled[c] - mass * accel_ref[c]
    acc = None
    for t in range(0, slave_ref.shape[0], 8):
        sl = slice(t, t + 8)
        found = lookup(state_rows(x_ref, vn_ref, rows), slave_ref[sl, :])
        normal = [normal_ref[c, sl, :] for c in range(3)]
        along = sum(found[c] * normal[c] for c in range(3))
        speed = sum(found[3 + c] * normal[c] for c in range(3))
        slave_side[0, sl, :] = along
        slave_side[1, sl, :] = speed
        got = scatter_tile(slot_ref[sl, :], [along, speed], slot_rows, 2)
        acc = got if acc is None else acc + got
    for c, value in enumerate(unstack(acc, 2, slot_rows, 2)):
        put_slots(pay, c, value, each)
    for t in range(slot_rows // 8):
        sl = slice(t * 8, t * 8 + 8)
        coded = slot_tile(early_ref, 3, t, each)
        master = jnp.maximum(coded - 0.5, 0.0).astype(jnp.int32)
        normal = [slot_tile(early_ref, c, t, each) for c in range(3)]
        found = lookup(state_rows(x_ref, vn_ref, rows), master)
        along = sum(found[c] * normal[c] for c in range(3))
        speed = sum(found[3 + c] * normal[c] for c in range(3))
        master_side[0, sl, :] = along
        master_side[1, sl, :] = speed
        step = 8 // each
        for j in range(step):
            pay[t * step + j, 2 * each : 3 * each, :] = along[j * each : (j + 1) * each]
            pay[t * step + j, 3 * each : 4 * each, :] = speed[j * each : (j + 1) * each]
    greeted(peers)
    copies = [pltpu.make_async_copy(pay.at[me], back.at[me], own_sem)]
    copies += [send(pay.at[peer], back.at[me], pay_send.at[i], pay_recv.at[i], peer)
               for i, peer in enumerate(peers)]
    for copy in copies:
        copy.start()
    vals[0] = mass
    for c in range(3):
        vals[1 + c] = mass * x_ref[c]
    for copy in copies:
        copy.wait()
    total[...] = jnp.zeros_like(total)
    for t in range(slot_rows // 8):
        sl = slice(t * 8, t * 8 + 8)
        for c in range(2):
            table[c, sl, :] = slot_tile(back, 2 + c, t, each)
        coded = slot_tile(early_ref, 3, t, each)
        master = jnp.maximum(coded - 0.5, 0.0).astype(jnp.int32)
        normal = [slot_tile(early_ref, c, t, each) for c in range(3)]
        push = pushed(slot_tile(back, 0, t, each) - master_side[0, sl, :],
                      slot_tile(back, 1, t, each) - master_side[1, sl, :])
        push = jnp.where(coded > 0.5, push, 0.0)
        total[...] += scatter_tile(master, [-push * normal[c] for c in range(3)], rows, 2)
    acc = None
    for t in range(0, slave_ref.shape[0], 8):
        sl = slice(t, t + 8)
        found = lookup(
            table_rows([lambda r, c=c: table[c, r : r + 1, :] for c in range(2)], slot_rows),
            slot_ref[sl, :])
        push = pushed(slave_side[0, sl, :] - found[0], slave_side[1, sl, :] - found[1])
        got = scatter_tile(slave_ref[sl, :], [push * normal_ref[c, sl, :] for c in range(3)],
                           rows, 2)
        acc = got if acc is None else acc + got
    contact = unstack(total[...] + acc, 3, rows, 2)
    x = [x_ref[c] for c in range(3)]
    net = []
    for c in range(3):
        nv_ref[c] = vn_ref[c] + TIME_STEP * contact[c] / mass
        net.append(vals[4 + c] + contact[c])
        vals[4 + c] = net[c]
    vals[7] = x[1] * net[2] - x[2] * net[1]
    vals[8] = x[2] * net[0] - x[0] * net[2]
    vals[9] = x[0] * net[1] - x[1] * net[0]
    part_rows = sums.shape[1]
    acc = None
    for t in range(0, rows, 8):
        sl = slice(t, t + 8)
        got = scatter_tile(part_ref[sl, :], [vals[k, sl, :] for k in range(10)], part_rows, 2)
        acc = got if acc is None else acc + got
    for k, value in enumerate(unstack(acc, 10, part_rows, 2)):
        sums[k] = value
    place = 0
    for g, (low, width) in enumerate(groups):
        size = 2**width
        digit = (me // 2**low) % size
        base = me - digit * 2**low
        copies = [pltpu.make_async_copy(sums, held[g].at[digit], sum_own.at[g])]
        for o in range(1, size):
            peer = base + ((digit + o) % size) * 2**low
            copies.append(send(sums, held[g].at[digit], sum_send.at[place],
                               sum_recv.at[place], peer))
            place += 1
        for copy in copies:
            copy.start()
        for copy in copies:
            copy.wait()
        value = held[g][0]
        for k in range(1, size):
            value = value + held[g][k]
        sums[...] = value
    arrived[...] = sums[...]
    for r in range(part_rows):
        wide = min(L, PARTS_SIZE - r * L)
        at = slice(r * L, r * L + wide)
        got = [arrived[k, r : r + 1, 0:wide] for k in range(10)]
        own_mass = pmass_ref[0:1, at]
        mass_total = own_mass + got[0]
        centre = [(own_mass * pcentre_ref[c : c + 1, at] + got[1 + c]) / mass_total
                  for c in range(3)]
        force = got[4:7]
        swept = [centre[1] * force[2] - centre[2] * force[1],
                 centre[2] * force[0] - centre[0] * force[2],
                 centre[0] * force[1] - centre[1] * force[0]]
        for c in range(3):
            motion_ref[c : c + 1, at] = force[c] / mass_total
            motion_ref[3 + c : 4 + c, at] = (got[7 + c] - swept[c]) / pinertia_ref[c : c + 1, at]


VMEM = pl.BlockSpec(memory_space=pltpu.VMEM)
SMEM = pl.BlockSpec(memory_space=pltpu.SMEM)


def call(body, outs, scratch, specs, name, collective=None):
    return pl.pallas_call(
        body,
        out_shape=outs,
        in_specs=specs,
        out_specs=[VMEM] * len(outs),
        scratch_shapes=scratch,
        name=name,
        compiler_params=pltpu.CompilerParams(
            vmem_limit_bytes=48 * 2**20, collective_id=collective,
            has_side_effects=collective is not None),
    )


def f32(*shape):
    return jax.ShapeDtypeStruct(shape, F32)


def per_device(rest_pos, displacement, velocity, ext_force, node_mass, body_accel, connectivity,
               elem_material, stiffness, shared_nodes, contact_slave, contact_owner,
               contact_master, contact_normal, part_of_node, part_mass, part_center,
               part_inertia):
    domains = lax.axis_size("dom")
    neighbours = shared_nodes.shape[1]
    nodes = displacement.shape[1]
    rows = nodes // L
    contacts = contact_slave.shape[0]
    tiles = contacts // L
    each = -(-(4 * contacts // domains) // L)
    slot_rows = domains * each
    part_rows = -(-PARTS_SIZE // L)
    dma = pltpu.SemaphoreType.DMA

    u = displacement.reshape(3, rows, L)
    v = velocity.reshape(3, rows, L)
    ext = ext_force.reshape(3, rows, L)
    rest = rest_pos.reshape(3, rows, L)
    mass = node_mass.reshape(rows, L)
    owner = contact_owner.reshape(tiles, L)
    master = contact_master.reshape(tiles, L)
    slave = contact_slave.reshape(tiles, L)
    normal = contact_normal.reshape(3, tiles, L)

    node_shape = f32(3, rows, L)
    rec_shape = f32(neighbours, 8, L)
    work = [pltpu.VMEM((3, rows, L), F32), pltpu.VMEM((6 * rows, L), F32),
            pltpu.VMEM((neighbours, 8, L), F32)]
    near = [dma((neighbours,))] * 2
    far = [dma((domains - 1,))] * 2 + [dma]
    materials, side = stiffness.shape[:2]
    internal, received, matrix, slot, early = call(
        functools.partial(first_body, each),
        [node_shape, rec_shape, jax.ShapeDtypeStruct((materials, side, 80), BF16),
         jax.ShapeDtypeStruct((tiles, L), jnp.int32), f32(domains, 4 * each, L)],
        work + [pltpu.VMEM((domains, 4 * each, L), F32)] + near + far,
        [VMEM] * 4 + [SMEM] + [VMEM] * 4, "first", 0)(
            u, v, connectivity, shared_nodes, elem_material, stiffness, owner, master, normal)
    for cycle in range(1, CYCLES):
        internal, received, u, v = call(
            next_body, [node_shape, rec_shape, node_shape, node_shape], work + near,
            [VMEM] * 4 + [SMEM] + [VMEM] * 5 + [SMEM], "next", 1)(
                u, v, connectivity, shared_nodes, elem_material, matrix, internal, received, ext,
                mass, body_accel)
    groups = bit_groups(domains)
    count = sum(2**width - 1 for _, width in groups)
    sum_shape = (10, part_rows, L)
    nodal_velocity, part_motion = call(
        functools.partial(last_body, each), [node_shape, f32(6, PARTS_SIZE)],
        [pltpu.VMEM((3, rows, L), F32)] * 2
        + [pltpu.VMEM((domains, 4 * each, L), F32)] * 2
        + [pltpu.VMEM((2, tiles, L), F32), pltpu.VMEM((2, slot_rows, L), F32),
           pltpu.VMEM((2, slot_rows, L), F32), pltpu.VMEM((10, rows, L), F32),
           pltpu.VMEM((6 * rows, L), F32), pltpu.VMEM(sum_shape, F32),
           pltpu.VMEM((2**groups[0][1],) + sum_shape, F32), pltpu.VMEM(sum_shape, F32)]
        + [pltpu.VMEM((2**width,) + sum_shape, F32) for _, width in groups[1:]]
        + far + [dma((count,))] * 2 + [dma((len(groups),))],
        [VMEM] * 7 + [SMEM] + [VMEM] * 9, "last", 2)(
            u, v, shared_nodes, internal, received, ext, mass, body_accel, rest, slave, slot,
            normal, early, part_of_node.reshape(rows, L), part_mass.reshape(1, PARTS_SIZE),
            part_center, part_inertia)
    return nodal_velocity.reshape(3, nodes), part_motion


def solution(mesh):
    placed = (
        P(None, "dom"), P(None, "dom"), P(None, "dom"), P(None, "dom"), P("dom"), P(),
        P(None, "dom"), P("dom"), P(), P("dom", None, None), P("dom"), P("dom", None), P("dom"),
        P(None, "dom"), P("dom"), P(), P(), P(),
    )
    return jax.shard_map(
        per_device, mesh=mesh, in_specs=placed, out_specs=(P(None, "dom"), P()), check_vma=False
    )
```

```python
import functools

import jax
import jax.numpy as jnp
from jax import lax
from jax.experimental import pallas as pl
from jax.experimental.pallas import tpu as pltpu
from jax.sharding import PartitionSpec as P

CYCLES = 3
PARTS_SIZE = 400
TIME_STEP = 0.1
DAMP_RATIO = 0.05
PENALTY = 2.0
GAP_WIDTH = 0.5
CONTACT_DAMP = 0.2
L = 128
GROUP = 4
F32 = jnp.float32
BF16 = jnp.bfloat16
NT = (((1,), (1,)), ((), ()))


def lookup(tables, index):
    high = index >> 7
    low = index & 127
    found = [None] * len(tables[0])
    for r, rows in enumerate(tables):
        hit = high == r
        for c, row in enumerate(rows):
            got = jnp.take_along_axis(
                jnp.broadcast_to(row, index.shape), low, axis=1, mode="promise_in_bounds"
            )
            found[c] = got if found[c] is None else jnp.where(hit, got, found[c])
    return found


def table_rows(refs, rows):
    return [[ref(r) for ref in refs] for r in range(rows)]


def spread(ref, row, count, *lead):
    one = jnp.broadcast_to(ref[(*lead, pl.ds(row, 1), slice(None))], (16, L)).astype(BF16)
    return jnp.concatenate([one] * (count // 16), 0) if count > 16 else one


def counting(rows):
    return lax.broadcasted_iota(jnp.int32, (rows, L), 0).astype(F32).astype(BF16)


def onehot_dot(count, rows, high, low, parts):
    height = max(rows, 16)
    sublane, place = counting(height), counting(L)
    one, zero = jnp.ones((), BF16), jnp.zeros((), BF16)
    left, right = [], []
    for s in range(count):
        mine = sublane == high(s, height)
        left.append(jnp.concatenate([jnp.where(mine, part(s, height), zero) for part in parts], 0))
        right.append(jnp.where(place == low(s, L), one, zero))
    return lax.dot_general(
        jnp.concatenate(left, 1), jnp.concatenate(right, 1), NT, preferred_element_type=F32)


def scatter_tile(index, values, rows, planes, slot, live=8):
    planes[slot, 0] = (index >> 7).astype(F32)
    planes[slot, 1] = (index & 127).astype(F32)
    for k, value in enumerate(values):
        value = jnp.concatenate(value, 0) if isinstance(value, list) else value
        top = value.astype(BF16).astype(F32)
        planes[slot, 2 + 2 * k, 0 : value.shape[0]] = top
        planes[slot, 3 + 2 * k, 0 : value.shape[0]] = value - top

    def row(k):
        return lambda s, height: spread(planes, s, height, slot, k)

    return onehot_dot(live, rows, row(0), row(1), [row(2 + k) for k in range(2 * len(values))])


def unstack(total, count, rows, pieces):
    out = []
    step = max(rows, 16)
    for c in range(count):
        base = c * pieces * step
        value = total[base : base + rows]
        for p in range(1, pieces):
            value = value + total[base + p * step : base + p * step + rows]
        out.append(value)
    return out


def advance(u, v, internal, received, shared, ext, mass, accel, rows, neighbours, planes):
    got = scatter_tile(shared, received, rows, planes, 0, neighbours)
    added = unstack(got, 3, rows, 2)
    assembled = [internal[c] + added[c] for c in range(3)]
    v = [v[c] + TIME_STEP * ((ext[c] - assembled[c]) / mass - accel[c]) for c in range(3)]
    u = [u[c] + TIME_STEP * v[c] for c in range(3)]
    return u, v, assembled


def by_part(rec_ref):
    return [[rec_ref[b, c : c + 1, :] for b in range(rec_ref.shape[0])] for c in range(3)]


def field_lookup(field, index):
    rows = field.shape[1]
    return lookup(
        table_rows([lambda r, c=c: field[c, r : r + 1, :] for c in range(3)], rows), index)


def prepare_corners(conn_ref, corner, high_ref, low_ref, nodes):
    for b in range(conn_ref.shape[1] // L):
        at = slice(b * L, (b + 1) * L)
        index = conn_ref[:, at] + (lax.broadcasted_iota(jnp.int32, (8, L), 1) + b * L)
        index = lax.rem(index, nodes)
        corner[:, at] = index
        high_ref[b * 8 : (b + 1) * 8, :] = (index >> 7).astype(F32)
        low_ref[b * 8 : (b + 1) * 8, :] = (index & 127).astype(F32)


def split_matrix(stiff_ref, matrix_ref):
    for m in range(stiff_ref.shape[0]):
        k = stiff_ref[m]
        k_hi = k.astype(BF16).astype(F32)
        matrix_ref[m] = jnp.concatenate(
            [k_hi, k_hi, k - k_hi, jnp.zeros((k.shape[0], 8), F32)], 1).astype(BF16)


def internal_forces(field, total, corner, high_ref, low_ref, material_ref, matrix_ref, pieces):
    rows = field.shape[1]
    total[...] = jnp.zeros_like(total)
    groups = corner.shape[1] // L // GROUP

    def group(i, slot):
        for k in range(GROUP):
            b = i * GROUP + k
            g = jnp.concatenate(
                field_lookup(field, corner[:, pl.ds(pl.multiple_of(b * L, L), L)]), 0)
            g_hi = g.astype(BF16).astype(F32)
            rhs = jnp.concatenate(
                [g_hi, g - g_hi, g_hi, jnp.zeros((8, L), F32)], 0).astype(BF16)
            h = jnp.dot(matrix_ref[material_ref[b]], rhs, preferred_element_type=F32)
            h_hi = h.astype(BF16).astype(F32)
            pieces[slot, 0, k * 24 : (k + 1) * 24, :] = h_hi
            pieces[slot, 1, k * 24 : (k + 1) * 24, :] = h - h_hi

    def add_group(i, slot):
        base = i * GROUP * 8

        def part(c, p):
            return lambda s, height: spread(
                pieces, (s // 8) * 24 + c * 8 + s % 8, height, slot, p)

        total[...] += onehot_dot(
            GROUP * 8, rows, lambda s, height: spread(high_ref, base + s, height),
            lambda s, height: spread(low_ref, base + s, height),
            [part(c, p) for c in range(3) for p in range(2)])

    def step(i, carry):
        group(2 * i + 1, 1)
        add_group(2 * i, 0)
        group(2 * i + 2, 0)
        add_group(2 * i + 1, 1)
        return carry

    group(0, 0)
    lax.fori_loop(0, groups // 2 - 1, step, 0)
    group(groups - 1, 1)
    add_group(groups - 2, 0)
    add_group(groups - 1, 1)
    return unstack(total[...], 3, rows, 2)


def shared_index(shared_ref):
    neighbours = shared_ref.shape[1]
    return jnp.concatenate(
        [shared_ref[0], jnp.zeros((8 - neighbours, shared_ref.shape[2]), jnp.int32)], 0)


def coords(index):
    return {"dom": index}


def greet(peers):
    barrier = pltpu.get_barrier_semaphore()
    for peer in peers:
        pl.semaphore_signal(barrier, inc=1, device_id=coords(peer),
                            device_id_type=pl.DeviceIdType.MESH)


def greeted(peers):
    pl.semaphore_wait(pltpu.get_barrier_semaphore(), len(peers))


def send(source, target, send_sem, recv_sem, peer):
    return pltpu.make_async_remote_copy(
        src_ref=source, dst_ref=target, send_sem=send_sem, recv_sem=recv_sem,
        device_id=coords(peer), device_id_type=pl.DeviceIdType.MESH)


def flips(me, neighbours):
    return [me + (1 - 2 * ((me // 2**b) % 2)) * 2**b for b in range(neighbours)]


def own_copies(own, rec_ref, send_sem, recv_sem, peers):
    return [send(own.at[b], rec_ref.at[b], send_sem.at[b], recv_sem.at[b], peer)
            for b, peer in enumerate(peers)]


def put_slots(ref, at, value, each):
    for d in range(ref.shape[0]):
        ref[d, at * each : (at + 1) * each, :] = value[d * each : (d + 1) * each]


def slot_tile(ref, at, tile, each):
    step = 8 // each
    return jnp.concatenate(
        [ref[tile * step + j, at * each : (at + 1) * each, :] for j in range(step)], 0)


def slots(owner_ref, master_ref, normal_ref, slot_ref, pay, each, planes):
    domains = pay.shape[0]
    tiles = owner_ref.shape[0]
    cap = each * L
    slot_rows = domains * each
    domain = lax.broadcasted_iota(jnp.int32, (domains, L), 0)
    tri = (lax.broadcasted_iota(jnp.int32, (L, L), 0) <= lax.broadcasted_iota(
        jnp.int32, (L, L), 1)).astype(F32).astype(BF16)
    seen = jnp.zeros((domains, 1), F32)
    for t in range(tiles):
        owner = owner_ref[t : t + 1, :]
        hit = domain == jnp.broadcast_to(owner, (domains, L))
        hits = jnp.where(hit, 1.0, 0.0)
        upto = jnp.dot(hits.astype(BF16), tri, preferred_element_type=F32) + seen
        rank = jnp.sum(jnp.where(hit, upto, 0.0), axis=0, keepdims=True) - 1.0
        slot_ref[t : t + 1, :] = owner * cap + rank.astype(jnp.int32)
        seen = seen + jnp.sum(hits, axis=1, keepdims=True)
    acc = None
    for t in range(0, tiles, 8):
        sl = slice(t, t + 8)
        values = [normal_ref[c, sl, :] for c in range(3)] + [master_ref[sl, :].astype(F32) + 1.0]
        got = scatter_tile(slot_ref[sl, :], values, slot_rows, planes, t // 8 % 4)
        acc = got if acc is None else acc + got
    for c, value in enumerate(unstack(acc, 4, slot_rows, 2)):
        put_slots(pay, c, value, each)


def state_rows(x_ref, v_ref, rows):
    return table_rows(
        [lambda r, c=c: x_ref[c, r : r + 1, :] for c in range(3)]
        + [lambda r, c=c: v_ref[c, r : r + 1, :] for c in range(3)], rows)


def pushed(gap, closing):
    z = -gap / GAP_WIDTH
    soft = jnp.maximum(z, 0.0) + jnp.log1p(jnp.exp(-jnp.abs(z)))
    return PENALTY * GAP_WIDTH * soft - CONTACT_DAMP * closing


def bit_groups(domains):
    bits = domains.bit_length() - 1
    groups, low = [], 0
    while low < bits:
        width = min(3, bits - low)
        if bits - low == 4:
            width = 2
        groups.append((low, width))
        low += width
    return groups


def part_sums(part_ref, vals, which, sums, planes):
    part_rows = sums.shape[1]
    acc = None
    for t in range(0, part_ref.shape[0], 8):
        sl = slice(t, t + 8)
        got = scatter_tile(
            part_ref[sl, :], [vals[k, sl, :] for k in which], part_rows, planes, t // 8 % 4)
        acc = got if acc is None else acc + got
    for k, value in zip(which, unstack(acc, len(which), part_rows, 2)):
        sums[k] = value


def window_body(each, u_ref, v_ref, rest_ref, ext_ref, mass_ref, accel_ref, conn_ref,
                material_ref, stiff_ref, shared_ref, slave_ref, owner_ref, master_ref, normal_ref,
                part_ref, pmass_ref, pcentre_ref, pinertia_ref, nv_ref, motion_ref, field, total,
                corner, high_ref, low_ref, pieces, matrix_ref, planes, own, rec, x_ref, vn_ref,
                slot_ref, ready, early_ref, pay, back, slave_side, master_side, table, vals, sums,
                first, *scratch):
    domains = pay.shape[0]
    groups = bit_groups(domains)
    held = (first,) + tuple(scratch[:len(groups) - 1])
    (near_send, near_recv, early_send, early_recv, early_own, pay_send, pay_recv, own_sem,
     sum_send, sum_recv, sum_own) = scratch[len(groups) - 1:]
    rows = u_ref.shape[1]
    slot_rows = domains * each
    neighbours = shared_ref.shape[1]
    me = lax.axis_index("dom")
    near = flips(me, neighbours)
    peers = [lax.rem(me + apart, domains) for apart in range(1, domains)]
    greet(peers)
    prepare_corners(conn_ref, corner, high_ref, low_ref, rows * L)
    split_matrix(stiff_ref, matrix_ref)
    shared = shared_index(shared_ref)
    mass = mass_ref[...]
    u = [u_ref[c] for c in range(3)]
    v = [v_ref[c] for c in range(3)]
    for cycle in range(CYCLES):
        for c in range(3):
            x_ref[c] = u[c]
            vn_ref[c] = v[c]
            field[c] = u[c] + DAMP_RATIO * v[c]
        internal = internal_forces(
            field, total, corner, high_ref, low_ref, material_ref, matrix_ref, pieces)
        for c in range(3):
            field[c] = internal[c]
        found = field_lookup(field, shared)
        for b in range(neighbours):
            for c in range(3):
                own[cycle, b, c : c + 1, :] = found[c][b : b + 1, :]
        if cycle == 0:
            greeted(peers)
        copies = [send(own.at[cycle, b], rec.at[cycle, b], near_send.at[cycle, b],
                       near_recv.at[cycle, b], peer) for b, peer in enumerate(near)]
        for copy in copies:
            copy.start()
        if cycle == 0:
            slots(owner_ref, master_ref, normal_ref, slot_ref, ready, each, planes)
        for copy in copies:
            copy.wait()
        if cycle == 0:
            early = [pltpu.make_async_copy(ready.at[me], early_ref.at[me], early_own)]
            early += [send(ready.at[peer], early_ref.at[me], early_send.at[i], early_recv.at[i],
                           peer) for i, peer in enumerate(peers)]
            for copy in early:
                copy.start()
        u, v, assembled = advance(
            [x_ref[c] for c in range(3)], [vn_ref[c] for c in range(3)],
            [field[c] for c in range(3)], by_part(rec.at[cycle]), shared,
            [ext_ref[c] for c in range(3)], mass, [accel_ref[c] for c in range(3)],
            rows, neighbours, planes)
    for c in range(3):
        x_ref[c] = rest_ref[c] + u[c]
        vn_ref[c] = v[c]
        vals[4 + c] = ext_ref[c] - assembled[c] - mass * accel_ref[c]
    for copy in early:
        copy.wait()
    acc = None
    for t in range(0, slave_ref.shape[0], 8):
        sl = slice(t, t + 8)
        found = lookup(state_rows(x_ref, vn_ref, rows), slave_ref[sl, :])
        normal = [normal_ref[c, sl, :] for c in range(3)]
        along = sum(found[c] * normal[c] for c in range(3))
        speed = sum(found[3 + c] * normal[c] for c in range(3))
        slave_side[0, sl, :] = along
        slave_side[1, sl, :] = speed
        got = scatter_tile(slot_ref[sl, :], [along, speed], slot_rows, planes, t // 8 % 4)
        acc = got if acc is None else acc + got
    for c, value in enumerate(unstack(acc, 2, slot_rows, 2)):
        put_slots(pay, c, value, each)
    for t in range(slot_rows // 8):
        sl = slice(t * 8, t * 8 + 8)
        coded = slot_tile(early_ref, 3, t, each)
        master = jnp.maximum(coded - 0.5, 0.0).astype(jnp.int32)
        normal = [slot_tile(early_ref, c, t, each) for c in range(3)]
        found = lookup(state_rows(x_ref, vn_ref, rows), master)
        along = sum(found[c] * normal[c] for c in range(3))
        speed = sum(found[3 + c] * normal[c] for c in range(3))
        master_side[0, sl, :] = along
        master_side[1, sl, :] = speed
        step = 8 // each
        for j in range(step):
            pay[t * step + j, 2 * each : 3 * each, :] = along[j * each : (j + 1) * each]
            pay[t * step + j, 3 * each : 4 * each, :] = speed[j * each : (j + 1) * each]
    copies = [pltpu.make_async_copy(pay.at[me], back.at[me], own_sem)]
    copies += [send(pay.at[peer], back.at[me], pay_send.at[i], pay_recv.at[i], peer)
               for i, peer in enumerate(peers)]
    for copy in copies:
        copy.start()
    vals[0] = mass
    for c in range(3):
        vals[1 + c] = mass * x_ref[c]
    part_rows = sums.shape[1]
    part_sums(part_ref, vals, range(4), sums, planes)
    for copy in copies:
        copy.wait()
    total[...] = jnp.zeros_like(total)
    for t in range(slot_rows // 8):
        sl = slice(t * 8, t * 8 + 8)
        for c in range(2):
            table[c, sl, :] = slot_tile(back, 2 + c, t, each)
        coded = slot_tile(early_ref, 3, t, each)
        master = jnp.maximum(coded - 0.5, 0.0).astype(jnp.int32)
        normal = [slot_tile(early_ref, c, t, each) for c in range(3)]
        push = pushed(slot_tile(back, 0, t, each) - master_side[0, sl, :],
                      slot_tile(back, 1, t, each) - master_side[1, sl, :])
        push = jnp.where(coded > 0.5, push, 0.0)
        total[...] += scatter_tile(
            master, [-push * normal[c] for c in range(3)], rows, planes, t % 4)
    acc = None
    for t in range(0, slave_ref.shape[0], 8):
        sl = slice(t, t + 8)
        found = lookup(
            table_rows([lambda r, c=c: table[c, r : r + 1, :] for c in range(2)], slot_rows),
            slot_ref[sl, :])
        push = pushed(slave_side[0, sl, :] - found[0], slave_side[1, sl, :] - found[1])
        got = scatter_tile(slave_ref[sl, :], [push * normal_ref[c, sl, :] for c in range(3)],
                           rows, planes, t // 8 % 4)
        acc = got if acc is None else acc + got
    contact = unstack(total[...] + acc, 3, rows, 2)
    x = [x_ref[c] for c in range(3)]
    net = []
    for c in range(3):
        nv_ref[c] = vn_ref[c] + TIME_STEP * contact[c] / mass
        net.append(vals[4 + c] + contact[c])
        vals[4 + c] = net[c]
    vals[7] = x[1] * net[2] - x[2] * net[1]
    vals[8] = x[2] * net[0] - x[0] * net[2]
    vals[9] = x[0] * net[1] - x[1] * net[0]
    part_sums(part_ref, vals, range(4, 10), sums, planes)
    place = 0
    for g, (low, width) in enumerate(groups):
        size = 2**width
        digit = (me // 2**low) % size
        base = me - digit * 2**low
        copies = [pltpu.make_async_copy(sums, held[g].at[digit], sum_own.at[g])]
        for o in range(1, size):
            peer = base + ((digit + o) % size) * 2**low
            copies.append(send(sums, held[g].at[digit], sum_send.at[place],
                               sum_recv.at[place], peer))
            place += 1
        for copy in copies:
            copy.start()
        for copy in copies:
            copy.wait()
        value = held[g][0]
        for k in range(1, size):
            value = value + held[g][k]
        sums[...] = value
    for r in range(part_rows):
        wide = min(L, PARTS_SIZE - r * L)
        at = slice(r * L, r * L + wide)
        got = [sums[k, r : r + 1, 0:wide] for k in range(10)]
        own_mass = pmass_ref[0:1, at]
        mass_total = own_mass + got[0]
        centre = [(own_mass * pcentre_ref[c : c + 1, at] + got[1 + c]) / mass_total
                  for c in range(3)]
        force = got[4:7]
        swept = [centre[1] * force[2] - centre[2] * force[1],
                 centre[2] * force[0] - centre[0] * force[2],
                 centre[0] * force[1] - centre[1] * force[0]]
        for c in range(3):
            motion_ref[c : c + 1, at] = force[c] / mass_total
            motion_ref[3 + c : 4 + c, at] = (got[7 + c] - swept[c]) / pinertia_ref[c : c + 1, at]


VMEM = pl.BlockSpec(memory_space=pltpu.VMEM)
SMEM = pl.BlockSpec(memory_space=pltpu.SMEM)


def call(body, outs, scratch, specs, name, collective=None):
    return pl.pallas_call(
        body,
        out_shape=outs,
        in_specs=specs,
        out_specs=[VMEM] * len(outs),
        scratch_shapes=scratch,
        name=name,
        compiler_params=pltpu.CompilerParams(
            vmem_limit_bytes=48 * 2**20, collective_id=collective,
            has_side_effects=collective is not None),
    )


def f32(*shape):
    return jax.ShapeDtypeStruct(shape, F32)


def per_device(rest_pos, displacement, velocity, ext_force, node_mass, body_accel, connectivity,
               elem_material, stiffness, shared_nodes, contact_slave, contact_owner,
               contact_master, contact_normal, part_of_node, part_mass, part_center,
               part_inertia):
    domains = lax.axis_size("dom")
    neighbours = shared_nodes.shape[1]
    nodes = displacement.shape[1]
    rows = nodes // L
    contacts = contact_slave.shape[0]
    tiles = contacts // L
    each = -(-(4 * contacts // domains) // L)
    slot_rows = domains * each
    part_rows = -(-PARTS_SIZE // L)
    dma = pltpu.SemaphoreType.DMA

    u = displacement.reshape(3, rows, L)
    v = velocity.reshape(3, rows, L)
    ext = ext_force.reshape(3, rows, L)
    rest = rest_pos.reshape(3, rows, L)
    mass = node_mass.reshape(rows, L)
    owner = contact_owner.reshape(tiles, L)
    master = contact_master.reshape(tiles, L)
    slave = contact_slave.reshape(tiles, L)
    normal = contact_normal.reshape(3, tiles, L)


    materials, side = stiffness.shape[:2]
    groups = bit_groups(domains)
    count = sum(2**width - 1 for _, width in groups)
    sum_shape = (10, part_rows, L)
    blocks = connectivity.shape[1] // L
    node = pltpu.VMEM((3, rows, L), F32)
    near = pltpu.VMEM((CYCLES, neighbours, 8, L), F32)
    payload = pltpu.VMEM((domains, 4 * each, L), F32)
    far = [dma((domains - 1,))] * 2 + [dma]
    nodal_velocity, part_motion = call(
        functools.partial(window_body, each), [f32(3, rows, L), f32(6, PARTS_SIZE)],
        [node, pltpu.VMEM((6 * rows, L), F32), pltpu.VMEM(connectivity.shape, jnp.int32),
         pltpu.VMEM((blocks * 8, L), F32), pltpu.VMEM((blocks * 8, L), F32),
         pltpu.VMEM((2, 2, 24 * GROUP, L), F32), pltpu.VMEM((materials, side, 80), BF16),
         pltpu.VMEM((4, 22, 8, L), F32), near, near, node, node,
         pltpu.VMEM((tiles, L), jnp.int32), payload, payload, payload, payload,
         pltpu.VMEM((2, tiles, L), F32), pltpu.VMEM((2, slot_rows, L), F32),
         pltpu.VMEM((2, slot_rows, L), F32), pltpu.VMEM((10, rows, L), F32),
         pltpu.VMEM(sum_shape, F32)]
        + [pltpu.VMEM((2**width,) + sum_shape, F32) for _, width in groups]
        + [dma((CYCLES, neighbours))] * 2 + far + far
        + [dma((count,))] * 2 + [dma((len(groups),))],
        [VMEM] * 5 + [SMEM, VMEM, SMEM] + [VMEM] * 10, "window", 0)(
            u, v, rest, ext, mass, body_accel, connectivity, elem_material, stiffness,
            shared_nodes, slave, owner, master, normal, part_of_node.reshape(rows, L),
            part_mass.reshape(1, PARTS_SIZE), part_center, part_inertia)
    return nodal_velocity.reshape(3, nodes), part_motion


def solution(mesh):
    placed = (
        P(None, "dom"), P(None, "dom"), P(None, "dom"), P(None, "dom"), P("dom"), P(),
        P(None, "dom"), P("dom"), P(), P("dom", None, None), P("dom"), P("dom", None), P("dom"),
        P(None, "dom"), P("dom"), P(), P(), P(),
    )
    return jax.shard_map(
        per_device, mesh=mesh, in_specs=placed, out_specs=(P(None, "dom"), P()), check_vma=False
    )
```
